32 devices in a mesh: dp: 16 (over z, y, core), mp: 2 (over x).
Axes of the slice: x: 2, y: 2, z: 4, core: 2. Of those that a mesh axis runs over, the one named last changes fastest.
Arguments:
- dino_tokens: bfloat16 [8192, 1024], P('dp', 'mp'), may hold values from -6 to 6
- siglip_tokens: bfloat16 [8192, 1152], P('dp', 'mp'), may hold values from -6 to 6
- dino_norm_one: float32 [1024], replicated, may hold values from 0.25 to 1.75
- dino_qkv: bfloat16 [1024, 3, 1024], P('dp', None, 'mp'), may hold values from -6.05625 to 6.05625
- dino_out: bfloat16 [1024, 1024], P('mp', 'dp'), may hold values from -0.1875 to 0.1875
- dino_norm_two: float32 [1024], replicated, may hold values from 0.25 to 1.75
- dino_up: bfloat16 [1024, 4096], P('dp', 'mp'), may hold values from -0.1875 to 0.1875
- dino_down: bfloat16 [4096, 1024], P('mp', 'dp'), may hold values from -0.09375 to 0.09375
- siglip_norm_one: float32 [1152], replicated, may hold values from 0.25 to 1.75
- siglip_qkv: bfloat16 [1152, 3, 1152], P('dp', None, 'mp'), may hold values from -5.709887 to 5.709887
- siglip_out: bfloat16 [1152, 1152], P('mp', 'dp'), may hold values from -0.1875 to 0.1875
- siglip_norm_two: float32 [1152], replicated, may hold values from 0.25 to 1.75
- siglip_up: bfloat16 [1152, 4304], P('dp', 'mp'), may hold values from -0.1875 to 0.1875
- siglip_down: bfloat16 [4304, 1152], P('mp', 'dp'), may hold values from -0.09375 to 0.09375
Outputs:
- dino_result: bfloat16 [8192, 1024], P('dp', 'mp')
- siglip_result: bfloat16 [8192, 1152], P('dp', 'mp')
The draws below stay inside these ranges and needn't reach their ends.
All inputs are finite; a program needn't handle non-finite values.
Results may differ from the reference program's by a relative error of at most 0.012.
Values may be sent and summed in bfloat16 or wider, within the bound.
No kernel may reach another device: no remote copies, remote signals or barrier semaphores. Data moves between devices by JAX's collectives and lax.ppermute only.
A program may use at most 128 MiB of HBM per device.

```python
import math
import jax
import jax.numpy as jnp
from jax import lax

D_DINO = 1024
FF_DINO = 4096
D_SIG = 1152
FF_SIG = 4304
HEADS = 16
PATCHES = 256
TOKENS = 8192


def qkv_law(key, width):
    first = jax.random.fold_in(key, 0)
    limit = 6.0 * width ** (-0.5)
    base = jnp.clip(jax.random.normal(first, (width, 3, width), jnp.float32) * width ** (-0.5), -limit, limit)
    return base


def draw_dino_qkv(key, part):
    return qkv_law(jax.random.fold_in(key, 11), D_DINO).astype(jnp.bfloat16)


def draw_siglip_qkv(key, part):
    return qkv_law(jax.random.fold_in(key, 23), D_SIG).astype(jnp.bfloat16)


def levels(rng, shape, cuts, low, high):
    factor_of, own = 1.0, jax.random.fold_in(rng, 6)
    for axis_at, shards_of in cuts:
        steps = jnp.exp(jax.random.uniform(jax.random.fold_in(own, axis_at), (shards_of,), jnp.float32, low / len(cuts), high / len(cuts)))
        factor_of = factor_of * jnp.repeat(steps, shape[axis_at] // shards_of).reshape([-1 if axis == axis_at else 1 for axis in range(len(shape))])
    return factor_of


def centred(own_key, extent, scale, reach, shards=(), held_as=jnp.bfloat16):
    drawn = scale * jax.random.normal(own_key, extent, jnp.float32)
    if shards:
        drawn = drawn * levels(own_key, extent, shards, -0.22, 0.18)
    return jnp.clip(drawn, -reach, reach).astype(held_as)


def setup_inputs(seed: int = 0) -> dict:
    arg_keys = jax.random.split(jax.random.key(seed), 15)
    return {
        "dino_tokens": centred(arg_keys[0], (TOKENS, D_DINO), 1.0, 6.0, ((0, 16), (1, 2))),
        "siglip_tokens": centred(arg_keys[1], (TOKENS, D_SIG), 1.0, 6.0, ((0, 16), (1, 2))),
        "dino_norm_one": jnp.clip(1.0 + 0.15 * jax.random.normal(arg_keys[2], (D_DINO,), jnp.float32), 0.25, 1.75),
        "dino_qkv": draw_dino_qkv(jax.random.fold_in(arg_keys[14], 71), 0),
        "dino_out": centred(arg_keys[4], (D_DINO, D_DINO), D_DINO ** -0.5, 0.1875, ((0, 2), (1, 16))),
        "dino_norm_two": jnp.clip(1.0 + 0.15 * jax.random.normal(arg_keys[5], (D_DINO,), jnp.float32), 0.25, 1.75),
        "dino_up": centred(arg_keys[6], (D_DINO, FF_DINO), D_DINO ** -0.5, 0.1875, ((0, 16), (1, 2))),
        "dino_down": centred(arg_keys[7], (FF_DINO, D_DINO), FF_DINO ** -0.5, 0.09375, ((0, 2), (1, 16))),
        "siglip_norm_one": jnp.clip(1.0 + 0.15 * jax.random.normal(arg_keys[8], (D_SIG,), jnp.float32), 0.25, 1.75),
        "siglip_qkv": draw_siglip_qkv(jax.random.fold_in(arg_keys[14], 71), 0),
        "siglip_out": centred(arg_keys[10], (D_SIG, D_SIG), D_SIG ** -0.5, 0.1875, ((0, 2), (1, 16))),
        "siglip_norm_two": jnp.clip(1.0 + 0.15 * jax.random.normal(arg_keys[11], (D_SIG,), jnp.float32), 0.25, 1.75),
        "siglip_up": centred(arg_keys[12], (D_SIG, FF_SIG), D_SIG ** -0.5, 0.1875, ((0, 16), (1, 2))),
        "siglip_down": centred(arg_keys[13], (FF_SIG, D_SIG), FF_SIG ** -0.5, 0.09375, ((0, 2), (1, 16))),
    }


EPS = 1e-06

def layer_norm(values, gain):
    values = values.astype(jnp.float32)
    center = values - lax.optimization_barrier(jnp.mean(values, axis=-1, keepdims=True))
    spread = lax.optimization_barrier(jnp.mean(center * center, axis=-1, keepdims=True))
    return (center * lax.rsqrt(spread + EPS) * gain.astype(jnp.float32)).astype(jnp.bfloat16)

def encode(block, norm_one, qkv_weight, out_weight, norm_two, up_weight, down_weight, approx):
    rows, width = block.shape
    head_size = width // HEADS
    scale = 1.0 / math.sqrt(head_size)
    normed = layer_norm(block, norm_one)
    qkv = jnp.dot(normed, qkv_weight.reshape(width, 3 * width), preferred_element_type=jnp.float32).astype(jnp.bfloat16)
    qkv = qkv.reshape(rows // PATCHES, PATCHES, 3, HEADS, head_size).astype(jnp.float32)
    query = qkv[:, :, 0]
    keys = qkv[:, :, 1]
    values = qkv[:, :, 2]
    scores = jnp.einsum('fqhd,fkhd->fhqk', query, keys) * scale
    top = lax.optimization_barrier(jnp.max(scores, axis=-1, keepdims=True))
    expo = jnp.exp(scores - top)
    probs = (expo / lax.optimization_barrier(jnp.sum(expo, axis=-1, keepdims=True))).astype(jnp.bfloat16)
    context = jnp.einsum('fhqk,fkhd->fqhd', probs.astype(jnp.float32), values)
    context = context.astype(jnp.bfloat16).reshape(rows, width)
    attended = jnp.dot(context, out_weight, preferred_element_type=jnp.float32)
    middle = (block.astype(jnp.float32) + attended).astype(jnp.bfloat16)
    second = layer_norm(middle, norm_two)
    hidden = jax.nn.gelu(jnp.dot(second, up_weight, preferred_element_type=jnp.float32), approximate=approx).astype(jnp.bfloat16)
    mixed = jnp.dot(hidden, down_weight, preferred_element_type=jnp.float32)
    return (middle.astype(jnp.float32) + mixed).astype(jnp.bfloat16)

def run_encoder(tokens, weights, approx):
    width = tokens.shape[1]
    blocks = tokens.reshape(-1, 8 * PATCHES, width)
    result = lax.map(lambda block: encode(block, *weights, approx), blocks)
    return result.reshape(tokens.shape)

def reference(dino_tokens, siglip_tokens, dino_norm_one, dino_qkv, dino_out, dino_norm_two, dino_up, dino_down, siglip_norm_one, siglip_qkv, siglip_out, siglip_norm_two, siglip_up, siglip_down):
    dino_result = run_encoder(dino_tokens, (dino_norm_one, dino_qkv, dino_out, dino_norm_two, dino_up, dino_down), False)
    siglip_result = run_encoder(siglip_tokens, (siglip_norm_one, siglip_qkv, siglip_out, siglip_norm_two, siglip_up, siglip_down), True)
    return (dino_result, siglip_result)
```

```python
import functools
import math

import jax
import jax.numpy as jnp
import numpy as np
from jax import lax
from jax.experimental import pallas as pl
from jax.experimental.pallas import tpu as pltpu
from jax.sharding import PartitionSpec as P


HEADS = 16
PATCHES = 256
EPS = 1e-06
LANES = 128
BLOCK = 256
BF16 = jnp.bfloat16
F32 = jnp.float32
MLP_VMEM = 24 * 2**20
NT = (((1,), (1,)), ((), ()))


def dot(a, b):
    return jnp.dot(a, b, preferred_element_type=F32)


def dot_nt(a, b):
    return lax.dot_general(a, b, NT, preferred_element_type=F32)


def gelu(x, approx):
    if approx:
        inner = math.sqrt(2.0 / math.pi) * (x + 0.044715 * (x * x * x))
        return 0.5 * x * (1.0 + jnp.tanh(inner))
    return 0.5 * x * (1.0 + lax.erf(x * math.sqrt(0.5)))


def layer_norm(values, gain):
    values = values.astype(F32)
    center = values - jnp.mean(values, axis=-1, keepdims=True)
    spread = jnp.mean(center * center, axis=-1, keepdims=True)
    return (center * lax.rsqrt(spread + EPS) * gain).astype(BF16)


def pack_attention(qkv, out):
    local = qkv.shape[2]
    main = local // LANES * LANES
    parts = [qkv[:, 0], qkv[:, 1], qkv[:, 2], out.T]
    packed = [p[:, :main] for p in parts]
    if main < local:
        packed[3:3] = [p[:, main:] for p in parts]
    return jnp.concatenate(packed, axis=1)


def project_kernel(count, local, turned, table, own_ref, other_ref, gain_ref, *rest):
    weights = rest[:count]
    weight, whole, projected, normed, sems = rest[count:]
    main = local // LANES * LANES
    extra = local - main
    part = weights[0].shape[0]

    def copy(at):
        start = pl.multiple_of(table[at] * part, 8)
        return pltpu.make_async_copy(
            weights[at], weight.at[pl.ds(start, part), :], sems.at[at]
        )

    for at in range(count):
        copy(at).start()
    rows = whole.shape[0]
    first = lax.axis_index("mp") == 0

    def load(ref, at):
        if not turned:
            return ref[pl.ds(at, PATCHES), :].astype(F32)
        values = ref[:, pl.ds(at, PATCHES)].astype(F32)
        half = values.shape[0]
        spare = -half % LANES
        if spare:
            values = jnp.concatenate([values, jnp.zeros((spare, PATCHES), F32)], axis=0)
        return values.T[:, :half]

    def norm_frame(f, _):
        at = pl.multiple_of(f * PATCHES, PATCHES)
        own, other = load(own_ref, at), load(other_ref, at)
        halves = [jnp.where(first, own, other), jnp.where(first, other, own)]
        values = jnp.concatenate(halves, axis=1)
        whole[pl.ds(at, PATCHES), :] = values.astype(BF16)
        normed[pl.ds(at, PATCHES), :] = layer_norm(values, gain_ref[...])
        return 0

    lax.fori_loop(0, rows // PATCHES, norm_frame, 0)
    for at in range(count):
        copy(at).wait()

    columns = 3 * main + (2 * LANES if extra else 0)
    step = 2 * BLOCK
    for lo in range(0, columns, step):
        size = min(step, columns - lo)
        piece = dot(normed[...], weight[:, lo : lo + size])
        projected[:, lo : lo + size] = piece.astype(BF16)


def attend_kernel(local, heads, weight, whole, projected, mine_ref, send_ref, context):
    main = local // LANES * LANES
    extra = local - main
    head = local // heads
    rows = whole.shape[0]

    def frame(f, _):
        at = pl.multiple_of(f * PATCHES, PATCHES)

        def tile(column):
            return projected[pl.ds(at, PATCHES), column : column + LANES]

        tiles = [[tile(j * main + t * LANES) for t in range(main // LANES)] for j in range(3)]
        if extra:
            left = tile(3 * main)
            tiles[0].append(left)
            turned = pltpu.roll(left.astype(F32), LANES - extra, 1)
            tiles[1].append(turned.astype(BF16))
            tiles[2].append(tile(3 * main + LANES))
        lane = lax.broadcasted_iota(jnp.int32, (PATCHES, LANES), 1)
        context_tiles = [None] * len(tiles[0])
        for h in range(heads):
            lo, hi = h * head, (h + 1) * head
            used = list(range(lo // LANES, (hi - 1) // LANES + 1))
            masks = [(lane >= lo - t * LANES) & (lane < hi - t * LANES) for t in used]
            query = [
                jnp.where(mask, tiles[0][t], jnp.zeros_like(tiles[0][t]))
                for t, mask in zip(used, masks)
            ]
            keys = [tiles[1][t] for t in used]
            values = [tiles[2][t] for t in used]
            cat = lambda xs: xs[0] if len(xs) == 1 else jnp.concatenate(xs, axis=1)
            scores = dot_nt(cat(query), cat(keys))
            top = jnp.max(scores, axis=-1, keepdims=True)
            expo = jnp.exp((scores - top) * (1.0 / math.sqrt(head)))
            share = 1.0 / jnp.sum(expo, axis=-1, keepdims=True)
            mixed = dot(expo.astype(BF16), cat(values)) * share
            for k, (t, mask) in enumerate(zip(used, masks)):
                now = mixed[:, k * LANES : (k + 1) * LANES]
                before = jnp.zeros_like(now) if context_tiles[t] is None else context_tiles[t]
                context_tiles[t] = jnp.where(mask, now, before)
        first = 0
        if extra:
            last = pltpu.roll(context_tiles.pop(), LANES - extra, 1)
            context[pl.ds(at, PATCHES), :LANES] = last.astype(BF16)
            first = LANES
        for t, piece in enumerate(context_tiles):
            lo = first + t * LANES
            context[pl.ds(at, PATCHES), lo : lo + LANES] = piece.astype(BF16)
        return 0

    lax.fori_loop(0, rows // PATCHES, frame, 0)
    lo = 3 * main + (LANES if extra else 0)
    size = main + (LANES if extra else 0)
    total = dot_nt(context[...], weight[:, lo : lo + size])
    send_ref[...] = total.astype(BF16)
    mine_ref[...] = total + whole[...].astype(F32)


def project(own, other, gain, weights, table, local, turned):
    rows, half = own.shape[::-1] if turned else own.shape
    width = 2 * half
    columns = weights[0].shape[1]
    count = len(weights)
    main = local // LANES * LANES
    extra = LANES if main < local else 0
    vmem = pl.BlockSpec(memory_space=pltpu.VMEM)
    anyspace = pl.BlockSpec(memory_space=pl.ANY)
    return pl.pallas_call(
        functools.partial(project_kernel, count, local, turned),
        out_shape=(
            pltpu.VMEM((width, columns), BF16),
            pltpu.VMEM((rows, width), BF16),
            pltpu.VMEM((rows, 3 * main + extra * 2), BF16),
        ),
        grid_spec=pltpu.PrefetchScalarGridSpec(
            num_scalar_prefetch=1,
            grid=(),
            in_specs=[vmem] * 3 + [anyspace] * count,
            out_specs=(vmem,) * 3,
            scratch_shapes=[
                pltpu.VMEM((rows, width), BF16),
                pltpu.SemaphoreType.DMA((count,)),
            ],
        ),
        compiler_params=pltpu.CompilerParams(vmem_limit_bytes=MLP_VMEM),
    )(table, own, other, gain.reshape(1, width), *weights)


def attention(weight, whole, projected, local, heads):
    rows, width = whole.shape
    size = -(-local // LANES) * LANES
    vmem = pl.BlockSpec(memory_space=pltpu.VMEM)
    return pl.pallas_call(
        functools.partial(attend_kernel, local, heads),
        out_shape=(
            jax.ShapeDtypeStruct((rows, width), F32),
            jax.ShapeDtypeStruct((rows, width), BF16),
        ),
        in_specs=[vmem] * 3,
        out_specs=(vmem, vmem),
        scratch_shapes=[pltpu.VMEM((rows, size), BF16)],
        compiler_params=pltpu.CompilerParams(vmem_limit_bytes=MLP_VMEM),
    )(weight, whole, projected)


def middle_kernel(turned, mine_ref, got_ref, gain_ref, second_ref, mid_ref):
    rows = mine_ref.shape[0]
    half = mine_ref.shape[1] // 2
    first = lax.axis_index("mp") == 0
    for at in range(0, rows, PATCHES):
        span = slice(at, at + PATCHES)
        total = mine_ref[span, :] + got_ref[span, :].astype(F32)
        middle = total.astype(BF16).astype(F32)
        second_ref[span, :] = layer_norm(middle, gain_ref[...])
        own = jnp.where(first, middle[:, :half], middle[:, half:])
        if turned:
            spare = -half % LANES
            if spare:
                own = jnp.concatenate([own, jnp.zeros((PATCHES, spare), F32)], axis=1)
            mid_ref[:, span] = own.T[:half, :].astype(BF16)
        else:
            mid_ref[span, :] = own.astype(BF16)


def middle(mine, got, gain, turned):
    rows, width = mine.shape
    half = width // 2
    vmem = pl.BlockSpec(memory_space=pltpu.VMEM)
    return pl.pallas_call(
        functools.partial(middle_kernel, turned),
        out_shape=(
            jax.ShapeDtypeStruct((rows, width), BF16),
            jax.ShapeDtypeStruct((half, rows) if turned else (rows, half), BF16),
        ),
        in_specs=[vmem] * 3,
        out_specs=(vmem, vmem),
        compiler_params=pltpu.CompilerParams(vmem_limit_bytes=MLP_VMEM),
    )(mine, got, gain.reshape(1, width))


def pack_mlp(up, down):
    spare = -up.shape[1] % LANES
    both = jnp.concatenate([up, down.T], axis=0)
    return jnp.pad(both, ((0, 0), (0, spare))) if spare else both


def weight_copies(table, sources, first, targets, sems):
    r = targets[0].shape[1]
    return [
        [
            pltpu.make_async_copy(
                source.at[pl.ds(k * r, r), :],
                target.at[table[first + i]],
                sems.at[k * len(sources) + i],
            )
            for i, source in enumerate(sources)
        ]
        for k, target in enumerate(targets)
    ]


def load_kernel(count, table, *refs):
    up, down, sems = refs[count:]
    copies = sum(weight_copies(table, refs[:count], 0, (up, down), sems), [])
    for c in copies:
        c.start()
    for c in copies:
        c.wait()


def flat(ref):
    return ref.reshape(ref.shape[0] * ref.shape[1], ref.shape[2])


def raise_to(approx, tokens_ref, up_ref, hidden_ref, lo, hi):
    for at in range(lo, hi, 2 * BLOCK):
        end = min(at + 2 * BLOCK, hi)
        raised = dot(tokens_ref[...], up_ref[:, at:end])
        hidden_ref[:, at:end] = gelu(raised, approx).astype(BF16)


def lower(hidden_ref, down, which, turned):
    half = down.shape[0] * down.shape[1] // 2
    at = pl.multiple_of(which * half, 8)
    weight = flat(down)[pl.ds(at, half), :]
    if turned:
        return dot_nt(weight, hidden_ref[...])
    return dot_nt(hidden_ref[...], weight)


def lower_other(hidden_ref, down, sent, send_ref, sem, turned):
    sent[...] = lower(hidden_ref, down, 1 - lax.axis_index("mp"), turned).astype(BF16)
    out = pltpu.make_async_copy(sent, send_ref, sem)
    out.start()
    out.wait()


def mlp_kernel(approx, turned, count, first, table, tokens_ref, *refs):
    sources = refs[2 : 2 + count]
    send_ref, hidden_ref, up, down, sent, sems = refs[2 + count :]
    copies = weight_copies(table, sources, first, (up, down), sems)
    for c in sum(copies, []):
        c.start()
    for c in copies[0]:
        c.wait()
    raise_to(approx, tokens_ref, flat(up), hidden_ref, 0, up.shape[2])
    for c in copies[1]:
        c.wait()
    lower_other(hidden_ref, down, sent, send_ref, sems.at[2 * count], turned)


def finish_kernel(*refs):
    for e in range(2):
        hidden_ref, mid_ref, down = refs[3 * e : 3 * e + 3]
        total = lower(hidden_ref, down, lax.axis_index("mp"), e == 1)
        refs[6 + e][...] = mid_ref[...].astype(F32) + total


def load(weights, table, width):
    r, columns = weights[0].shape[0] // 2, weights[0].shape[1]
    count = len(weights)
    shape = pltpu.VMEM((width // r, r, columns), BF16)
    vmem = pl.BlockSpec(memory_space=pltpu.VMEM)
    anyspace = pl.BlockSpec(memory_space=pl.ANY)
    return pl.pallas_call(
        functools.partial(load_kernel, count),
        out_shape=(shape, shape),
        grid_spec=pltpu.PrefetchScalarGridSpec(
            num_scalar_prefetch=1,
            grid=(),
            in_specs=[anyspace] * count,
            out_specs=(vmem, vmem),
            scratch_shapes=[pltpu.SemaphoreType.DMA((2 * count,))],
        ),
        compiler_params=pltpu.CompilerParams(vmem_limit_bytes=MLP_VMEM),
    )(table, *weights)


def mlp(tokens, loaded, weights, first, table, approx, turned):
    rows, width = tokens.shape
    count = len(weights)
    shape = loaded[0].shape
    sent = (width // 2, rows) if turned else (rows, width // 2)
    vmem = pl.BlockSpec(memory_space=pltpu.VMEM)
    anyspace = pl.BlockSpec(memory_space=pl.ANY)
    send, hidden, _, down = pl.pallas_call(
        functools.partial(mlp_kernel, approx, turned, count, first),
        out_shape=(
            pltpu.HBM(sent, BF16),
            pltpu.VMEM((rows, shape[2]), BF16),
            pltpu.VMEM(shape, BF16),
            pltpu.VMEM(shape, BF16),
        ),
        grid_spec=pltpu.PrefetchScalarGridSpec(
            num_scalar_prefetch=1,
            grid=(),
            in_specs=[vmem] * 3 + [anyspace] * count,
            out_specs=(anyspace, vmem, vmem, vmem),
            scratch_shapes=[
                pltpu.VMEM(sent, BF16),
                pltpu.SemaphoreType.DMA((2 * count + 1,)),
            ],
        ),
        input_output_aliases={2: 2, 3: 3},
        compiler_params=pltpu.CompilerParams(vmem_limit_bytes=MLP_VMEM),
    )(table, tokens, *loaded, *weights)
    return send, hidden, down


def finish(hidden_values, mids, downs):
    vmem = pl.BlockSpec(memory_space=pltpu.VMEM)
    operands = [x for e in range(2) for x in (hidden_values[e], mids[e], downs[e])]
    return pl.pallas_call(
        finish_kernel,
        out_shape=tuple(jax.ShapeDtypeStruct(x.shape, F32) for x in mids),
        in_specs=[vmem] * 6,
        out_specs=(vmem, vmem),
        compiler_params=pltpu.CompilerParams(vmem_limit_bytes=MLP_VMEM),
        name="finish",
    )(*operands)


def swap_mp(x):
    return lax.ppermute(x, "mp", [(0, 1), (1, 0)])


def ring_order(chips):
    return [0] + list(range(1, chips, 2)) + list(range(chips - 2, 0, -2))


class Ring:
    def __init__(self, n):
        chips = n // 2
        order = ring_order(chips)
        after = {order[i]: order[(i + 1) % chips] for i in range(chips)}
        before = {v: k for k, v in after.items()}
        self.hop = [(2 * c, 2 * after[c]) for c in range(chips)]
        self.hop += [(2 * c + 1, 2 * before[c] + 1) for c in range(chips)]
        self.core = [(d, d ^ 1) for d in range(n)]
        self.hops = chips - 1
        source = {b: a for a, b in self.hop}
        owners = list(range(n))
        self.tables = []
        for _ in range(chips):
            self.tables += [owners, [owners[d ^ 1] for d in range(n)]]
            owners = [owners[source[d]] for d in range(n)]

    def both(self, x):
        return [x, lax.ppermute(x, "dp", self.core)]

    def step(self, x):
        return lax.ppermute(x, "dp", self.hop)


def local(
    mesh_sizes,
    dino_tokens,
    siglip_tokens,
    dino_norm_one,
    dino_qkv,
    dino_out,
    dino_norm_two,
    dino_up,
    dino_down,
    siglip_norm_one,
    siglip_qkv,
    siglip_out,
    siglip_norm_two,
    siglip_up,
    siglip_down,
):
    n, groups = mesh_sizes
    d = lax.axis_index("dp")
    heads = HEADS // groups
    tokens = [dino_tokens, siglip_tokens.T]
    others = [swap_mp(x) for x in tokens]
    packed = [pack_attention(dino_qkv, dino_out), pack_attention(siglip_qkv, siglip_out)]
    locals_ = [dino_qkv.shape[2], siglip_qkv.shape[2]]
    shards = [pack_mlp(dino_up, dino_down), pack_mlp(siglip_up, siglip_down)]
    direct = direct_ring(n)
    if direct:
        assert all(p.shape[0] % 8 == 0 for p in packed)
    gots, mines = [], []

    def attend(e, weights):
        state = project(tokens[e], others[e], ones[e], weights, table, locals_[e], e == 1)
        mine, send = attention(*state, locals_[e], heads)
        mines.append(mine)
        gots.append(swap_mp(send))

    ones = [dino_norm_one, siglip_norm_one]
    twos = [dino_norm_two, siglip_norm_two]
    if direct:
        ring = Ring(n)
        table = jnp.array(np.array(ring.tables, np.int32).T)
        table = lax.dynamic_index_in_dim(table, d, 0, keepdims=False)
        streams = [packed, shards]
        gathered = []
        for stage, now in enumerate(streams):
            now = list(now)
            gathered.append([ring.both(x) for x in now])
            for h in range(ring.hops):
                if (stage, h) == (0, 2):
                    now[0] = lax.optimization_barrier((now[0], table))[0]
                for e in range(2):
                    now[e] = ring.step(now[e])
                    gathered[-1][e] += ring.both(now[e])
        for e in range(2):
            attend(e, gathered[0][e])
    else:
        table = jnp.zeros((1,), jnp.int32)
        gather = lambda x: lax.all_gather(x, "dp", axis=0, tiled=True)
        for e in range(2):
            attend(e, [gather(packed[e])])
        ups, downs = [dino_up, siglip_up], [dino_down.T, siglip_down.T]
        gathered = [None, [[pack_mlp(gather(u), gather(v).T)] for u, v in zip(ups, downs)]]
    mids, seconds = [], []
    for e in range(2):
        second, mid = middle(mines[e], gots[e], twos[e], e == 1)
        seconds.append(second)
        mids.append(mid)
    sends, hidden_values, downs = [], [], []
    for e in range(2):
        shards = gathered[1][e]
        first = max(len(shards) - 2, 1)
        loaded = load(shards[:first], table, seconds[e].shape[1])
        send, hidden, down = mlp(seconds[e], loaded, shards[first:], first, table, e == 1, e == 1)
        sends.append(swap_mp(send))
        hidden_values.append(hidden)
        downs.append(down)
    mines = finish(hidden_values, mids, downs)
    results = [(mines[e] + sends[e].astype(F32)).astype(BF16) for e in range(2)]
    return results[0], results[1].T


def direct_ring(n):
    return 8 <= n <= 16


def solution(mesh):
    in_specs = (
        P("dp", "mp"),
        P("dp", "mp"),
        P(),
        P("dp", None, "mp"),
        P("mp", "dp"),
        P(),
        P("dp", "mp"),
        P("mp", "dp"),
        P(),
        P("dp", None, "mp"),
        P("mp", "dp"),
        P(),
        P("dp", "mp"),
        P("mp", "dp"),
    )
    out_specs = (P("dp", "mp"), P("dp", "mp"))
    sizes = (mesh.shape["dp"], mesh.shape["mp"])

    def body(*args):
        return local(sizes, *args)

    return jax.shard_map(body, mesh=mesh, in_specs=in_specs, out_specs=out_specs, check_vma=False)
```

```python
import functools
import math

import jax
import jax.numpy as jnp
import numpy as np
from jax import lax
from jax.experimental import pallas as pl
from jax.experimental.pallas import tpu as pltpu
from jax.sharding import PartitionSpec as P


HEADS = 16
PATCHES = 256
EPS = 1e-06
LANES = 128
BLOCK = 256
BF16 = jnp.bfloat16
F32 = jnp.float32
MLP_VMEM = 24 * 2**20
NT = (((1,), (1,)), ((), ()))


def dot(a, b):
    return jnp.dot(a, b, preferred_element_type=F32)


def dot_nt(a, b):
    return lax.dot_general(a, b, NT, preferred_element_type=F32)


def gelu(x, approx):
    if approx:
        inner = math.sqrt(2.0 / math.pi) * (x + 0.044715 * (x * x * x))
        return 0.5 * x * (1.0 + jnp.tanh(inner))
    return 0.5 * x * (1.0 + lax.erf(x * math.sqrt(0.5)))


def layer_norm(values, gain):
    values = values.astype(F32)
    center = values - jnp.mean(values, axis=-1, keepdims=True)
    spread = jnp.mean(center * center, axis=-1, keepdims=True)
    return (center * lax.rsqrt(spread + EPS) * gain).astype(BF16)


def pack_attention(qkv, out):
    local = qkv.shape[2]
    main = local // LANES * LANES
    parts = [qkv[:, 0], qkv[:, 1], qkv[:, 2], out.T]
    packed = [p[:, :main] for p in parts]
    if main < local:
        packed[3:3] = [p[:, main:] for p in parts]
    return jnp.concatenate(packed, axis=1)


def project_kernel(count, local, turned, table, own_ref, other_ref, gain_ref, *rest):
    weights = rest[:count]
    weight, whole, projected, normed, sems = rest[count:]
    main = local // LANES * LANES
    extra = local - main
    part = weights[0].shape[0]

    def copy(at):
        start = pl.multiple_of(table[at] * part, 8)
        return pltpu.make_async_copy(
            weights[at], weight.at[pl.ds(start, part), :], sems.at[at]
        )

    for at in range(count):
        copy(at).start()
    rows = whole.shape[0]
    first = lax.axis_index("mp") == 0

    def load(ref, at):
        if not turned:
            return ref[pl.ds(at, PATCHES), :].astype(F32)
        values = ref[:, pl.ds(at, PATCHES)].astype(F32)
        half = values.shape[0]
        spare = -half % LANES
        if spare:
            values = jnp.concatenate([values, jnp.zeros((spare, PATCHES), F32)], axis=0)
        return values.T[:, :half]

    def norm_frame(f, _):
        at = pl.multiple_of(f * PATCHES, PATCHES)
        own, other = load(own_ref, at), load(other_ref, at)
        halves = [jnp.where(first, own, other), jnp.where(first, other, own)]
        values = jnp.concatenate(halves, axis=1)
        whole[pl.ds(at, PATCHES), :] = values.astype(BF16)
        normed[pl.ds(at, PATCHES), :] = layer_norm(values, gain_ref[...])
        return 0

    lax.fori_loop(0, rows // PATCHES, norm_frame, 0)
    for at in range(count):
        copy(at).wait()

    columns = 3 * main + (2 * LANES if extra else 0)
    step = 2 * BLOCK
    for lo in range(0, columns, step):
        size = min(step, columns - lo)
        piece = dot(normed[...], weight[:, lo : lo + size])
        projected[:, lo : lo + size] = piece.astype(BF16)


def attend_kernel(local, heads, weight, whole, projected, mine_ref, send_ref, context):
    main = local // LANES * LANES
    extra = local - main
    head = local // heads
    rows = whole.shape[0]

    def frame(f, _):
        at = pl.multiple_of(f * PATCHES, PATCHES)

        def tile(column):
            return projected[pl.ds(at, PATCHES), column : column + LANES]

        tiles = [[tile(j * main + t * LANES) for t in range(main // LANES)] for j in range(3)]
        if extra:
            left = tile(3 * main)
            tiles[0].append(left)
            turned = pltpu.roll(left.astype(F32), LANES - extra, 1)
            tiles[1].append(turned.astype(BF16))
            tiles[2].append(tile(3 * main + LANES))
        lane = lax.broadcasted_iota(jnp.int32, (PATCHES, LANES), 1)
        context_tiles = [None] * len(tiles[0])
        for h in range(heads):
            lo, hi = h * head, (h + 1) * head
            used = list(range(lo // LANES, (hi - 1) // LANES + 1))
            masks = [(lane >= lo - t * LANES) & (lane < hi - t * LANES) for t in used]
            query = [
                jnp.where(mask, tiles[0][t], jnp.zeros_like(tiles[0][t]))
                for t, mask in zip(used, masks)
            ]
            keys = [tiles[1][t] for t in used]
            values = [tiles[2][t] for t in used]
            cat = lambda xs: xs[0] if len(xs) == 1 else jnp.concatenate(xs, axis=1)
            scores = dot_nt(cat(query), cat(keys))
            top = jnp.max(scores, axis=-1, keepdims=True)
            expo = jnp.exp((scores - top) * (1.0 / math.sqrt(head)))
            share = 1.0 / jnp.sum(expo, axis=-1, keepdims=True)
            mixed = dot(expo.astype(BF16), cat(values)) * share
            for k, (t, mask) in enumerate(zip(used, masks)):
                now = mixed[:, k * LANES : (k + 1) * LANES]
                before = jnp.zeros_like(now) if context_tiles[t] is None else context_tiles[t]
                context_tiles[t] = jnp.where(mask, now, before)
        first = 0
        if extra:
            last = pltpu.roll(context_tiles.pop(), LANES - extra, 1)
            context[pl.ds(at, PATCHES), :LANES] = last.astype(BF16)
            first = LANES
        for t, piece in enumerate(context_tiles):
            lo = first + t * LANES
            context[pl.ds(at, PATCHES), lo : lo + LANES] = piece.astype(BF16)
        return 0

    lax.fori_loop(0, rows // PATCHES, frame, 0)
    lo = 3 * main + (LANES if extra else 0)
    size = main + (LANES if extra else 0)
    total = dot_nt(context[...], weight[:, lo : lo + size])
    send_ref[...] = total.astype(BF16)
    mine_ref[...] = total + whole[...].astype(F32)


def project(own, other, gain, weights, table, local, turned):
    rows, half = own.shape[::-1] if turned else own.shape
    width = 2 * half
    columns = weights[0].shape[1]
    count = len(weights)
    main = local // LANES * LANES
    extra = LANES if main < local else 0
    vmem = pl.BlockSpec(memory_space=pltpu.VMEM)
    anyspace = pl.BlockSpec(memory_space=pl.ANY)
    return pl.pallas_call(
        functools.partial(project_kernel, count, local, turned),
        out_shape=(
            pltpu.VMEM((width, columns), BF16),
            pltpu.VMEM((rows, width), BF16),
            pltpu.VMEM((rows, 3 * main + extra * 2), BF16),
        ),
        grid_spec=pltpu.PrefetchScalarGridSpec(
            num_scalar_prefetch=1,
            grid=(),
            in_specs=[vmem] * 3 + [anyspace] * count,
            out_specs=(vmem,) * 3,
            scratch_shapes=[
                pltpu.VMEM((rows, width), BF16),
                pltpu.SemaphoreType.DMA((count,)),
            ],
        ),
        compiler_params=pltpu.CompilerParams(vmem_limit_bytes=MLP_VMEM),
    )(table, own, other, gain.reshape(1, width), *weights)


def attention(weight, whole, projected, local, heads):
    rows, width = whole.shape
    size = -(-local // LANES) * LANES
    vmem = pl.BlockSpec(memory_space=pltpu.VMEM)
    return pl.pallas_call(
        functools.partial(attend_kernel, local, heads),
        out_shape=(
            jax.ShapeDtypeStruct((rows, width), F32),
            jax.ShapeDtypeStruct((rows, width), BF16),
        ),
        in_specs=[vmem] * 3,
        out_specs=(vmem, vmem),
        scratch_shapes=[pltpu.VMEM((rows, size), BF16)],
        compiler_params=pltpu.CompilerParams(vmem_limit_bytes=MLP_VMEM),
    )(weight, whole, projected)


def middle_kernel(turned, mine_ref, got_ref, gain_ref, second_ref, mid_ref):
    rows = mine_ref.shape[0]
    half = mine_ref.shape[1] // 2
    first = lax.axis_index("mp") == 0
    for at in range(0, rows, PATCHES):
        span = slice(at, at + PATCHES)
        total = mine_ref[span, :] + got_ref[span, :].astype(F32)
        middle = total.astype(BF16).astype(F32)
        second_ref[span, :] = layer_norm(middle, gain_ref[...])
        own = jnp.where(first, middle[:, :half], middle[:, half:])
        if turned:
            spare = -half % LANES
            if spare:
                own = jnp.concatenate([own, jnp.zeros((PATCHES, spare), F32)], axis=1)
            mid_ref[:, span] = own.T[:half, :].astype(BF16)
        else:
            mid_ref[span, :] = own.astype(BF16)


def middle(mine, got, gain, turned):
    rows, width = mine.shape
    half = width // 2
    vmem = pl.BlockSpec(memory_space=pltpu.VMEM)
    return pl.pallas_call(
        functools.partial(middle_kernel, turned),
        out_shape=(
            jax.ShapeDtypeStruct((rows, width), BF16),
            jax.ShapeDtypeStruct((half, rows) if turned else (rows, half), BF16),
        ),
        in_specs=[vmem] * 3,
        out_specs=(vmem, vmem),
        compiler_params=pltpu.CompilerParams(vmem_limit_bytes=MLP_VMEM),
    )(mine, got, gain.reshape(1, width))


def pack_mlp(up, down):
    spare = -up.shape[1] % LANES
    both = jnp.concatenate([up, down.T], axis=0)
    return jnp.pad(both, ((0, 0), (0, spare))) if spare else both


def weight_copies(table, sources, first, targets, sems):
    r = targets[0].shape[1]
    return [
        [
            pltpu.make_async_copy(
                source.at[pl.ds(k * r, r), :],
                target.at[table[first + i]],
                sems.at[k * len(sources) + i],
            )
            for i, source in enumerate(sources)
        ]
        for k, target in enumerate(targets)
    ]


def load_kernel(count, table, *refs):
    up, down, sems = refs[count:]
    copies = sum(weight_copies(table, refs[:count], 0, (up, down), sems), [])
    for c in copies:
        c.start()
    for c in copies:
        c.wait()


def flat(ref):
    return ref.reshape(ref.shape[0] * ref.shape[1], ref.shape[2])


def raise_to(approx, tokens_ref, up_ref, hidden_ref, lo, hi):
    for at in range(lo, hi, 2 * BLOCK):
        end = min(at + 2 * BLOCK, hi)
        raised = dot(tokens_ref[...], up_ref[:, at:end])
        hidden_ref[:, at:end] = gelu(raised, approx).astype(BF16)


def lower(hidden_ref, down, which, turned):
    half = down.shape[0] * down.shape[1] // 2
    at = pl.multiple_of(which * half, 8)
    weight = flat(down)[pl.ds(at, half), :]
    if turned:
        return dot_nt(weight, hidden_ref[...])
    return dot_nt(hidden_ref[...], weight)


def lower_other(hidden_ref, down, sent, send_ref, sem, turned):
    sent[...] = lower(hidden_ref, down, 1 - lax.axis_index("mp"), turned).astype(BF16)
    out = pltpu.make_async_copy(sent, send_ref, sem)
    out.start()
    out.wait()


def raise_kernel(approx, count, first, table, tokens_ref, *refs):
    sources = refs[2 : 2 + count]
    hidden_ref, up, down, sems = refs[2 + count :]
    copies = weight_copies(table, sources, first, (up, down), sems)
    for c in sum(copies, []):
        c.start()
    for c in copies[0]:
        c.wait()
    raise_to(approx, tokens_ref, flat(up), hidden_ref, 0, up.shape[2])
    for c in copies[1]:
        c.wait()


def lower_kernel(turned, hidden_ref, down, send_ref, sent, sem):
    lower_other(hidden_ref, down, sent, send_ref, sem.at[0], turned)


def finish_kernel(*refs):
    for e in range(2):
        hidden_ref, mid_ref, down = refs[3 * e : 3 * e + 3]
        total = lower(hidden_ref, down, lax.axis_index("mp"), e == 1)
        refs[6 + e][...] = mid_ref[...].astype(F32) + total


def load(weights, table, width):
    r, columns = weights[0].shape[0] // 2, weights[0].shape[1]
    count = len(weights)
    shape = pltpu.VMEM((width // r, r, columns), BF16)
    vmem = pl.BlockSpec(memory_space=pltpu.VMEM)
    anyspace = pl.BlockSpec(memory_space=pl.ANY)
    return pl.pallas_call(
        functools.partial(load_kernel, count),
        out_shape=(shape, shape),
        grid_spec=pltpu.PrefetchScalarGridSpec(
            num_scalar_prefetch=1,
            grid=(),
            in_specs=[anyspace] * count,
            out_specs=(vmem, vmem),
            scratch_shapes=[pltpu.SemaphoreType.DMA((2 * count,))],
        ),
        compiler_params=pltpu.CompilerParams(vmem_limit_bytes=MLP_VMEM),
    )(table, *weights)


def mlp_raise(tokens, loaded, weights, first, table, approx):
    rows = tokens.shape[0]
    count = len(weights)
    shape = loaded[0].shape
    vmem = pl.BlockSpec(memory_space=pltpu.VMEM)
    anyspace = pl.BlockSpec(memory_space=pl.ANY)
    hidden, _, down = pl.pallas_call(
        functools.partial(raise_kernel, approx, count, first),
        out_shape=(
            pltpu.VMEM((rows, shape[2]), BF16),
            pltpu.VMEM(shape, BF16),
            pltpu.VMEM(shape, BF16),
        ),
        grid_spec=pltpu.PrefetchScalarGridSpec(
            num_scalar_prefetch=1,
            grid=(),
            in_specs=[vmem] * 3 + [anyspace] * count,
            out_specs=(vmem,) * 3,
            scratch_shapes=[pltpu.SemaphoreType.DMA((max(2 * count, 1),))],
        ),
        input_output_aliases={2: 1, 3: 2},
        compiler_params=pltpu.CompilerParams(vmem_limit_bytes=MLP_VMEM),
    )(table, tokens, *loaded, *weights)
    return hidden, down


def mlp_lower(hidden, down, turned):
    rows, half = hidden.shape[0], down.shape[0] * down.shape[1] // 2
    sent = (half, rows) if turned else (rows, half)
    vmem = pl.BlockSpec(memory_space=pltpu.VMEM)
    return pl.pallas_call(
        functools.partial(lower_kernel, turned),
        out_shape=pltpu.HBM(sent, BF16),
        in_specs=[vmem, vmem],
        out_specs=pl.BlockSpec(memory_space=pl.ANY),
        scratch_shapes=[pltpu.VMEM(sent, BF16), pltpu.SemaphoreType.DMA((1,))],
        compiler_params=pltpu.CompilerParams(vmem_limit_bytes=MLP_VMEM),
    )(hidden, down)


def finish(hidden_values, mids, downs):
    vmem = pl.BlockSpec(memory_space=pltpu.VMEM)
    operands = [x for e in range(2) for x in (hidden_values[e], mids[e], downs[e])]
    return pl.pallas_call(
        finish_kernel,
        out_shape=tuple(jax.ShapeDtypeStruct(x.shape, F32) for x in mids),
        in_specs=[vmem] * 6,
        out_specs=(vmem, vmem),
        compiler_params=pltpu.CompilerParams(vmem_limit_bytes=MLP_VMEM),
        name="finish",
    )(*operands)


def swap_mp(x):
    return lax.ppermute(x, "mp", [(0, 1), (1, 0)])


def ring_order(chips):
    return [0] + list(range(1, chips, 2)) + list(range(chips - 2, 0, -2))


class Ring:
    def __init__(self, n):
        chips = n // 2
        order = ring_order(chips)
        after = {order[i]: order[(i + 1) % chips] for i in range(chips)}
        before = {v: k for k, v in after.items()}
        self.hop = [(2 * c, 2 * after[c]) for c in range(chips)]
        self.hop += [(2 * c + 1, 2 * before[c] + 1) for c in range(chips)]
        self.core = [(d, d ^ 1) for d in range(n)]
        self.hops = chips - 1
        source = {b: a for a, b in self.hop}
        owners = list(range(n))
        self.tables = []
        for _ in range(chips):
            self.tables += [owners, [owners[d ^ 1] for d in range(n)]]
            owners = [owners[source[d]] for d in range(n)]

    def both(self, x):
        return [x, lax.ppermute(x, "dp", self.core)]

    def step(self, x):
        return lax.ppermute(x, "dp", self.hop)


def local(
    mesh_sizes,
    dino_tokens,
    siglip_tokens,
    dino_norm_one,
    dino_qkv,
    dino_out,
    dino_norm_two,
    dino_up,
    dino_down,
    siglip_norm_one,
    siglip_qkv,
    siglip_out,
    siglip_norm_two,
    siglip_up,
    siglip_down,
):
    n, groups = mesh_sizes
    d = lax.axis_index("dp")
    heads = HEADS // groups
    tokens = [dino_tokens, siglip_tokens.T]
    others = [swap_mp(x) for x in tokens]
    packed = [pack_attention(dino_qkv, dino_out), pack_attention(siglip_qkv, siglip_out)]
    locals_ = [dino_qkv.shape[2], siglip_qkv.shape[2]]
    shards = [pack_mlp(dino_up, dino_down), pack_mlp(siglip_up, siglip_down)]
    direct = direct_ring(n)
    if direct:
        assert all(p.shape[0] % 8 == 0 for p in packed)
    gots, mines = [], []

    def attend(e, weights):
        state = project(tokens[e], others[e], ones[e], weights, table, locals_[e], e == 1)
        mine, send = attention(*state, locals_[e], heads)
        mines.append(mine)
        gots.append(swap_mp(send))

    ones = [dino_norm_one, siglip_norm_one]
    twos = [dino_norm_two, siglip_norm_two]
    if direct:
        ring = Ring(n)
        table = jnp.array(np.array(ring.tables, np.int32).T)
        table = lax.dynamic_index_in_dim(table, d, 0, keepdims=False)
        streams = [packed, shards]
        gathered = []
        for stage, now in enumerate(streams):
            now = list(now)
            gathered.append([ring.both(x) for x in now])
            for h in range(ring.hops):
                if (stage, h) == (0, 2):
                    now[0] = lax.optimization_barrier((now[0], table))[0]
                for e in range(2):
                    now[e] = ring.step(now[e])
                    gathered[-1][e] += ring.both(now[e])
        for e in range(2):
            attend(e, gathered[0][e])
    else:
        table = jnp.zeros((1,), jnp.int32)
        gather = lambda x: lax.all_gather(x, "dp", axis=0, tiled=True)
        for e in range(2):
            attend(e, [gather(packed[e])])
        ups, downs = [dino_up, siglip_up], [dino_down.T, siglip_down.T]
        gathered = [None, [[pack_mlp(gather(u), gather(v).T)] for u, v in zip(ups, downs)]]
    mids, seconds = [], []
    for e in range(2):
        second, mid = middle(mines[e], gots[e], twos[e], e == 1)
        seconds.append(second)
        mids.append(mid)
    sends, hidden_values, downs = [], [], []
    for e in range(2):
        shards = gathered[1][e]
        first = max(len(shards) - 2, 1)
        loaded = load(shards[:first], table, seconds[e].shape[1])
        hidden, down = mlp_raise(seconds[e], loaded, shards[first:], first, table, e == 1)
        send = mlp_lower(hidden, down, e == 1)
        sends.append(swap_mp(send))
        hidden_values.append(hidden)
        downs.append(down)
    mines = finish(hidden_values, mids, downs)
    results = [(mines[e] + sends[e].astype(F32)).astype(BF16) for e in range(2)]
    return results[0], results[1].T


def direct_ring(n):
    return 8 <= n <= 16


def solution(mesh):
    in_specs = (
        P("dp", "mp"),
        P("dp", "mp"),
        P(),
        P("dp", None, "mp"),
        P("mp", "dp"),
        P(),
        P("dp", "mp"),
        P("mp", "dp"),
        P(),
        P("dp", None, "mp"),
        P("mp", "dp"),
        P(),
        P("dp", "mp"),
        P("mp", "dp"),
    )
    out_specs = (P("dp", "mp"), P("dp", "mp"))
    sizes = (mesh.shape["dp"], mesh.shape["mp"])

    def body(*args):
        return local(sizes, *args)

    return jax.shard_map(body, mesh=mesh, in_specs=in_specs, out_specs=out_specs, check_vma=False)
```
